32 devices in a mesh: lon: 8 (over y, x, core), lat: 4 (over z).
Axes of the slice: x: 2, y: 2, z: 4, core: 2. Of those that a mesh axis runs over, the one named last changes fastest.
Arguments:
- state: float32 [3, 4, 256, 1024], P(None, None, 'lat', 'lon'), may hold values from -0.010253906 to 0.010253906
- depth: float32 [256, 1024], P('lat', 'lon'), may hold values from 0.1 to 1
- source_mask: int32 [8, 32], P('lat', 'lon'), may hold values 0 or 1
- gauge_lat: int32 [4], replicated, may hold values from 0 to 255
- gauge_lon: int32 [4], replicated, may hold values from 0 to 1023
- misfit: float32 [6, 4], replicated, may hold values from -4 to 4
Outputs:
- adjoint_state: float32 [3, 4, 256, 1024], P(None, None, 'lat', 'lon')
- coefficients: float32 [4, 512, 512], P(None, 'lon', 'lat')
The draws below stay inside these ranges and needn't reach their ends.
All inputs are finite; a program needn't handle non-finite values. No bound on the sum of `source_mask` on one device may be relied on, other than what follows from the above.
Results may differ from the reference program's by a relative error of at most 0.0003.
Values sent between devices are 32-bit elements; how exact they have to be, the bound alone decides.
A program may use at most 64 MiB of HBM per device.

```python
import math
import jax
import jax.numpy as jnp
from jax import lax

ADJ = 4
STEPS = 6
BLOCK = 32
KX = 512
KY = 512
NY = 256
NX = 1024


noise_level = 3.0


noise_bound = 3.5


def draw_state(key, part):
    scale = noise_level / NX
    shape = (3, ADJ, NY, NX)
    values = jnp.clip(jax.random.normal(key, shape, jnp.float32), -noise_bound, noise_bound)
    return (values * scale).astype(jnp.float32)


def set_ends(entries, stream_key, low, largest):
    extent = entries.shape
    place = [jax.random.randint(jax.random.fold_in(stream_key, axis), (), 0, extent[axis]) for axis in range(len(extent))]
    entries = entries.at[tuple(place)].set(low)
    longest = extent.index(max(extent))
    place[longest] = (place[longest] + 1) % extent[longest]
    return entries.at[tuple(place)].set(largest)


def level_of(key, dims, shards, least, high):
    def one(position, blocks):
        steps = jax.random.uniform(jax.random.fold_in(jax.random.fold_in(key, 6), position), (blocks,), jnp.float32, least / len(shards), high / len(shards))
        return jnp.repeat(jnp.exp(steps), dims[position] // blocks).reshape((-1,) + (1,) * (len(dims) - position - 1))

    level = one(*shards[0])
    for cut in shards[1:]:
        level = level * one(*cut)
    return level


def centred(rng, extent, deviation, most, held_as=jnp.bfloat16):
    result = jax.random.normal(rng, extent, jnp.float32) * deviation
    return jnp.minimum(jnp.maximum(result, -most), most).astype(held_as)


def setup_inputs(seed: int = 0) -> dict:
    seeds = jax.random.split(jax.random.key(seed), 7)
    return {
        "state": draw_state(jax.random.fold_in(seeds[6], 71), 0),
        "depth": jnp.clip(jnp.exp(math.log(1.0) - 2.3025851 * jax.random.uniform(seeds[1], (NY, NX), jnp.float32) ** level_of(seeds[1], (NY, NX), ((0, 4), (1, 8)), -0.2, 0.2)), 0.1, 1.0),
        "source_mask": set_ends((jax.random.randint(seeds[2], (NY // BLOCK, NX // BLOCK), 0, 2) < 1).astype(jnp.int32), jax.random.fold_in(seeds[2], 1), 0, 1),
        "gauge_lat": set_ends(jax.random.randint(seeds[3], (ADJ,), 0, NY), jax.random.fold_in(seeds[3], 1), 0, NY - 1).astype(jnp.int32),
        "gauge_lon": set_ends(jax.random.randint(seeds[4], (ADJ,), 0, NX), jax.random.fold_in(seeds[4], 1), 0, NX - 1).astype(jnp.int32),
        "misfit": centred(seeds[5], (STEPS, ADJ), 1.0, 4.0, jnp.float32),
    }


time_step = 0.5

def centred_x(f):
    return 0.5 * (f[..., 1:-1, 2:] - f[..., 1:-1, :-2])

def centred_y(f):
    return 0.5 * (f[..., 2:, 1:-1] - f[..., :-2, 1:-1])

def basis(total, modes, start, count):
    cells = start + jnp.arange(count, dtype=jnp.int32)
    order = jnp.arange(modes, dtype=jnp.int32)
    half = modes // 2
    wave = jnp.where(order < half, order, order - half + 1)
    phase = (cells[:, None] * wave[None, :] % total).astype(jnp.float32) * (2.0 * math.pi / total)
    return jnp.where(order[None, :] < half, jnp.cos(phase), jnp.sin(phase))

def reference(state, depth, source_mask, gauge_lat, gauge_lon, misfit):
    full_mask = jnp.repeat(jnp.repeat(source_mask, BLOCK, 0), BLOCK, 1).astype(jnp.float32)
    lat_basis = basis(NY, KY, 0, NY)
    lon_basis = basis(NX, KX, 0, NX)
    scale = 2.0 / math.sqrt(NX * NY)

    def one_adjoint(items):
        heights, east, north, row, col, pushes = items
        for step in range(STEPS):
            padded_east = jnp.pad(east, 1)
            padded_north = jnp.pad(north, 1)
            heights = heights + time_step * (centred_x(padded_east) + centred_y(padded_north))
            heights = heights.at[row, col].add(pushes[step])
            padded = jnp.pad(heights, 1)
            east = east + time_step * depth * centred_x(padded)
            north = north + time_step * depth * centred_y(padded)
        masked = heights * full_mask
        partial_sums = jnp.dot(lat_basis.T, masked, precision=lax.Precision.HIGHEST)
        modes = jnp.dot(partial_sums, lon_basis, precision=lax.Precision.HIGHEST).T * scale
        return (jnp.stack([heights, east, north]), modes)
    fields, modes = lax.map(one_adjoint, (state[0], state[1], state[2], gauge_lat, gauge_lon, misfit.T))
    return (jnp.transpose(fields, (1, 0, 2, 3)), modes)
```

```python
import functools
import math

import jax
import jax.numpy as jnp
import ml_dtypes
import numpy as np
from jax import lax
from jax.experimental import pallas as pl
from jax.experimental.pallas import tpu as pltpu
from jax.sharding import PartitionSpec as P

STEPS = 6
KX = 512
KY = 512
ADJ = 4
PAIRS = ADJ // 2
HALO = 16
SLOTS = 128 // HALO

MESH = pl.DeviceIdType.MESH
FLOAT = jnp.float32
HALF = jnp.bfloat16


def basis(total, modes):
    cells = np.arange(total, dtype=np.int64)
    order = np.arange(modes, dtype=np.int64)
    half = modes // 2
    wave = np.where(order < half, order, order - half + 1)
    phase = (cells[:, None] * wave[None, :] % total).astype(np.float64) * (2.0 * math.pi / total)
    return np.where(order[None, :] < half, np.cos(phase), np.sin(phase))


def halves(table):
    high = table.astype(ml_dtypes.bfloat16)
    low = (table - high.astype(np.float64)).astype(ml_dtypes.bfloat16)
    return high, low


def lon_table(total, count):
    table = basis(total, KX).T.reshape(KX, count, total // count).transpose(1, 0, 2)
    return np.stack(halves(table), axis=1)


def lat_table(total, count, scale):
    rows, own = total // count, KY // count
    table = (scale * basis(total, KY)).reshape(count, rows, count, own).transpose(2, 0, 1, 3)
    wide = np.zeros((count, count, 2, rows, 2, own))
    for member in range(2):
        wide[:, :, member, :, member] = table
    return np.stack(halves(wide.reshape(count, count * 2 * rows, 2 * own)), axis=1)


def split(x):
    high = x.astype(HALF)
    return high, (x - high.astype(FLOAT)).astype(HALF)


def turn(x, shift, axis):
    shift %= x.shape[axis]
    return x if shift == 0 else pltpu.roll(x, shift, axis)


def kernel(
    lon_count, lat_count,
    state, depth, source, gauge_lat, gauge_lon, misfit, lon_hbm, lat_hbm,
    fields, modes,
    ext, ext_depth, coef, gauges, pack_w, pack_e, got_e, got_w, lon_tab, lat_tab,
    part, pieces, gathered,
    halo_send, halo_recv, tab_sem, rs_send, rs_recv, ga_send, ga_recv,
):
    rows, cols = depth.shape
    high, wide = rows + 2 * HALO, 2 * cols
    own = modes.shape[1]
    lanes_out = modes.shape[2]
    lon = lax.axis_index("lon")
    lat = lax.axis_index("lat")
    has_e, has_w = lon < lon_count - 1, lon > 0
    has_n, has_s = lat < lat_count - 1, lat > 0

    tables = [
        pltpu.make_async_copy(lon_hbm.at[lon], lon_tab, tab_sem.at[0]),
        pltpu.make_async_copy(lat_hbm.at[lat], lat_tab, tab_sem.at[1]),
    ]
    for copy in tables:
        copy.start()

    corners = [
        (jnp.logical_and(has_e, has_n), 1, 1),
        (jnp.logical_and(has_e, has_s), 1, -1),
        (jnp.logical_and(has_w, has_n), -1, 1),
        (jnp.logical_and(has_w, has_s), -1, -1),
    ]
    barrier = pltpu.get_barrier_semaphore()
    for d in range(1, lon_count):
        pl.semaphore_signal(barrier, 1, device_id=(lax.rem(lon + d, lon_count), lat), device_id_type=MESH)
    for d in range(1, lat_count):
        pl.semaphore_signal(barrier, 1, device_id=(lon, lax.rem(lat + d, lat_count)), device_id_type=MESH)
    for there, dx, dy in corners:
        @pl.when(there)
        def _():
            pl.semaphore_signal(barrier, 1, device_id=(lon + dx, lat + dy), device_id_type=MESH)

    lane = lax.broadcasted_iota(jnp.int32, (rows, 128), 1)
    arrays = [state[f, a] for f in range(3) for a in range(ADJ)] + [depth[...]]
    for tile in range(2):
        west = jnp.zeros((rows, 128), FLOAT)
        east = west
        for slot in range(SLOTS):
            index = tile * SLOTS + slot
            if index < len(arrays):
                at = slot * HALO
                here = jnp.logical_and(lane >= at, lane < at + HALO)
                west = jnp.where(here, turn(arrays[index], at, 1), west)
                east = jnp.where(here, turn(arrays[index], at + HALO - cols, 1), east)
        pack_w[:, tile * 128:(tile + 1) * 128] = west
        pack_e[:, tile * 128:(tile + 1) * 128] = east

    diagonal = sum(there.astype(jnp.int32) for there, _, _ in corners)
    pl.semaphore_wait(barrier, lon_count - 1 + lat_count - 1 + diagonal)

    low = slice(0, HALO)
    top = slice(rows - HALO, rows)
    north = slice(rows, rows + HALO)
    south = slice(rows + HALO, high)
    every = slice(0, rows)
    plan = [
        (has_e, has_w, pack_e, got_w.at[every], 1, 0),
        (has_w, has_e, pack_w, got_e.at[every], -1, 0),
        (has_n, has_s, state.at[:, :, top], ext.at[:, :, south, 0:cols], 0, 1),
        (has_s, has_n, state.at[:, :, low], ext.at[:, :, north, 0:cols], 0, -1),
        (has_n, has_s, depth.at[top], ext_depth.at[south, 0:cols], 0, 1),
        (has_s, has_n, depth.at[low], ext_depth.at[north, 0:cols], 0, -1),
        (corners[0][0], corners[3][0], pack_e.at[top], got_w.at[south], 1, 1),
        (corners[1][0], corners[2][0], pack_e.at[low], got_w.at[north], 1, -1),
        (corners[2][0], corners[1][0], pack_w.at[top], got_e.at[south], -1, 1),
        (corners[3][0], corners[0][0], pack_w.at[low], got_e.at[north], -1, -1),
    ]

    def halo_copy(index):
        _, _, source_ref, target, dx, dy = plan[index]
        return pltpu.make_async_remote_copy(
            src_ref=source_ref, dst_ref=target,
            send_sem=halo_send.at[index], recv_sem=halo_recv.at[index],
            device_id=(lon + dx, lat + dy), device_id_type=MESH,
        )

    for index, (sends, gets, _, target, _, _) in enumerate(plan):
        @pl.when(sends)
        def _():
            halo_copy(index).start()

        @pl.when(jnp.logical_not(gets))
        def _():
            target[...] = jnp.zeros(target.shape, FLOAT)

    ext[:, :, 0:rows, 0:cols] = state[...]
    ext_depth[0:rows, 0:cols] = depth[...]
    row = lax.broadcasted_iota(jnp.int32, (high, wide), 0)
    col = lax.broadcasted_iota(jnp.int32, (high, wide), 1)
    row = lat * rows + jnp.where(row < rows + HALO, row, row - high)
    real = jnp.logical_or(col < cols + HALO, col >= wide - HALO)
    col = lon * cols + jnp.where(col < cols + HALO, col, col - wide)
    inside = (row >= 0) & (row < lat_count * rows) & (col >= 0) & (col < lon_count * cols) & real
    coef[0] = jnp.where(inside, 0.25, 0.0).astype(FLOAT)
    for a in range(ADJ):
        hit = (row == gauge_lat[a]) & (col == gauge_lon[a]) & real
        gauges[a] = jnp.where(hit, 1.0, 0.0).astype(FLOAT)
    line = lax.broadcasted_iota(jnp.int32, (rows, cols), 0)
    place = lax.broadcasted_iota(jnp.int32, (rows, cols), 1)
    mask = jnp.zeros((rows, cols), FLOAT)
    side = rows // source.shape[0]
    for i in range(source.shape[0]):
        for j in range(source.shape[1]):
            tile = (line >= i * side) & (line < (i + 1) * side) & (place >= j * side) & (place < (j + 1) * side)
            mask = jnp.where(tile, source[i, j].astype(FLOAT), mask)

    for index, (_, gets, _, _, _, _) in enumerate(plan):
        @pl.when(gets)
        def _():
            halo_copy(index).wait_recv()

    lane = lax.broadcasted_iota(jnp.int32, (high, 128), 1)

    def unpacked(index):
        tile, at = index // SLOTS, index % SLOTS * HALO
        span = slice(tile * 128, (tile + 1) * 128)
        right = turn(got_e[:, span], -at, 1)
        left = turn(got_w[:, span], -at - HALO, 1)
        return jnp.where(lane < HALO, right, jnp.where(lane >= 128 - HALO, left, 0.0))

    ext_depth[:, cols:wide] = unpacked(3 * ADJ)
    quarter = 0.25 * ext_depth[...]
    coef[1] = turn(quarter, -1, 1)
    coef[2] = turn(quarter, -1, 0)

    def rs_copy(p, d):
        target = lax.rem(lon + d, lon_count)
        return pltpu.make_async_remote_copy(
            src_ref=part.at[p, pl.ds(pl.multiple_of(target * own, own), own)],
            dst_ref=pieces.at[p, d - 1],
            send_sem=rs_send.at[p, d - 1], recv_sem=rs_recv.at[p, d - 1],
            device_id=(target, lat), device_id_type=MESH,
        )

    def ga_copy(p, d):
        return pltpu.make_async_remote_copy(
            src_ref=gathered.at[p, lat], dst_ref=gathered.at[p, lat],
            send_sem=ga_send.at[p, d - 1], recv_sem=ga_recv.at[p, d - 1],
            device_id=(lon, lax.rem(lat + d, lat_count)), device_id_type=MESH,
        )

    def ga_arrival(p, d):
        origin = lax.rem(lat + lat_count - d, lat_count)
        return pltpu.make_async_remote_copy(
            src_ref=gathered.at[p, origin], dst_ref=gathered.at[p, origin],
            send_sem=ga_send.at[p, d - 1], recv_sem=ga_recv.at[p, d - 1],
            device_id=(lon, origin), device_id_type=MESH,
        )

    for p in range(PAIRS):
        members = (2 * p, 2 * p + 1)
        for a in members:
            ext[0, a, :, cols:wide] = unpacked(a)
            ext[1, a, :, cols:wide] = unpacked(ADJ + a)
            ext[2, a, :, cols:wide] = unpacked(2 * ADJ + a)
            ext[1, a] = turn(ext[1, a], -1, 1)
            ext[2, a] = turn(ext[2, a], -1, 0)

        def step(t, carry):
            for a in members:
                east, north_ = ext[1, a], ext[2, a]
                change = (east - turn(east, 2, 1)) + (north_ - turn(north_, 2, 0))
                height = ext[0, a] + coef[0] * change + gauges[a] * misfit[t, a]
                ext[0, a] = height
                ext[1, a] = east + coef[1] * (turn(height, -2, 1) - height)
                ext[2, a] = north_ + coef[2] * (turn(height, -2, 0) - height)
            return carry

        lax.fori_loop(0, STEPS, step, 0)
        if p == 0:
            for copy in tables:
                copy.wait()
        masked = []
        for a in members:
            height = ext[0, a, 0:rows, 0:cols]
            masked.append(height * mask)
        high_m, low_m = split(jnp.concatenate(masked, axis=0))
        dims = (((1,), (1,)), ((), ()))
        part[p] = (
            lax.dot_general(lon_tab[0], high_m, dims, preferred_element_type=FLOAT)
            + lax.dot_general(lon_tab[0], low_m, dims, preferred_element_type=FLOAT)
            + lax.dot_general(lon_tab[1], high_m, dims, preferred_element_type=FLOAT)
        )
        for d in range(1, lon_count):
            rs_copy(p, d).start()
        for a in members:
            fields[0, a] = ext[0, a, 0:rows, 0:cols]
            fields[1, a] = turn(ext[1, a], 1, 1)[0:rows, 0:cols]
            fields[2, a] = turn(ext[2, a], 1, 0)[0:rows, 0:cols]

    for p in range(PAIRS):
        total = part[p, pl.ds(pl.multiple_of(lon * own, own), own)]
        for d in range(1, lon_count):
            rs_copy(p, d).wait_recv()
            total = total + pieces[p, d - 1]
        gathered[p, lat] = total
        for d in range(1, lat_count):
            ga_copy(p, d).start()

    for p in range(PAIRS):
        for d in range(1, lat_count):
            ga_arrival(p, d).wait_recv()
        high_g, low_g = split(jnp.concatenate([gathered[p, z] for z in range(lat_count)], axis=1))
        result = (
            jnp.dot(high_g, lat_tab[0], preferred_element_type=FLOAT)
            + jnp.dot(low_g, lat_tab[0], preferred_element_type=FLOAT)
            + jnp.dot(high_g, lat_tab[1], preferred_element_type=FLOAT)
        )
        for member in range(2):
            modes[2 * p + member] = result[:, member * lanes_out:(member + 1) * lanes_out]

    for index, (sends, _, _, _, _, _) in enumerate(plan):
        @pl.when(sends)
        def _():
            halo_copy(index).wait_send()
    for p in range(PAIRS):
        for d in range(1, lon_count):
            rs_copy(p, d).wait_send()
        for d in range(1, lat_count):
            ga_copy(p, d).wait_send()


def on_device(lon_count, lat_count, tables, state, depth, source_mask, gauge_lat, gauge_lon, misfit):
    rows, cols = depth.shape
    own_x, own_y = KX // lon_count, KY // lat_count
    high, wide = rows + 2 * HALO, 2 * cols
    vmem = pl.BlockSpec(memory_space=pltpu.VMEM)
    smem = pl.BlockSpec(memory_space=pltpu.SMEM)
    anywhere = pl.BlockSpec(memory_space=pl.ANY)
    dma = pltpu.SemaphoreType.DMA
    return pl.pallas_call(
        functools.partial(kernel, lon_count, lat_count),
        out_shape=(
            jax.ShapeDtypeStruct((3, ADJ, rows, cols), FLOAT),
            jax.ShapeDtypeStruct((ADJ, own_x, own_y), FLOAT),
        ),
        in_specs=[vmem, vmem, smem, smem, smem, smem, anywhere, anywhere],
        out_specs=(vmem, vmem),
        scratch_shapes=[
            pltpu.VMEM((3, ADJ, high, wide), FLOAT),
            pltpu.VMEM((high, wide), FLOAT),
            pltpu.VMEM((3, high, wide), FLOAT),
            pltpu.VMEM((ADJ, high, wide), FLOAT),
            pltpu.VMEM((rows, 256), FLOAT),
            pltpu.VMEM((rows, 256), FLOAT),
            pltpu.VMEM((high, 256), FLOAT),
            pltpu.VMEM((high, 256), FLOAT),
            pltpu.VMEM((2, KX, cols), HALF),
            pltpu.VMEM((2, lat_count * 2 * rows, 2 * own_y), HALF),
            pltpu.VMEM((PAIRS, KX, 2 * rows), FLOAT),
            pltpu.VMEM((PAIRS, lon_count - 1, own_x, 2 * rows), FLOAT),
            pltpu.VMEM((PAIRS, lat_count, own_x, 2 * rows), FLOAT),
            dma((10,)),
            dma((10,)),
            dma((2,)),
            dma((PAIRS, lon_count - 1)),
            dma((PAIRS, lon_count - 1)),
            dma((PAIRS, lat_count - 1)),
            dma((PAIRS, lat_count - 1)),
        ],
        compiler_params=pltpu.CompilerParams(
            collective_id=0, has_side_effects=True, vmem_limit_bytes=32 * 1024 * 1024
        ),
    )(state, depth, source_mask, gauge_lat, gauge_lon, misfit, *tables)


def solution(mesh):
    lon_count, lat_count = mesh.shape["lon"], mesh.shape["lat"]
    placed = (P(None, None, "lat", "lon"), P("lat", "lon"), P("lat", "lon"), P(), P(), P())

    def whole(state, depth, source_mask, gauge_lat, gauge_lon, misfit):
        total_rows, total_cols = depth.shape
        scale = 2.0 / math.sqrt(total_rows * total_cols)
        tables = (lon_table(total_cols, lon_count), lat_table(total_rows, lat_count, scale))

        def local(*args):
            constants = tuple(jnp.asarray(table) for table in tables)
            return on_device(lon_count, lat_count, constants, *args)

        return jax.shard_map(
            local,
            mesh=mesh,
            in_specs=placed,
            out_specs=(P(None, None, "lat", "lon"), P(None, "lon", "lat")),
            check_vma=False,
        )(state, depth, source_mask, gauge_lat, gauge_lon, misfit)

    return whole
```

```python
import functools
import math

import jax
import jax.numpy as jnp
import ml_dtypes
import numpy as np
from jax import lax
from jax.experimental import pallas as pl
from jax.experimental.pallas import tpu as pltpu
from jax.sharding import PartitionSpec as P

STEPS = 6
KX = 512
KY = 512
ADJ = 4
PAIRS = ADJ // 2
HALO = 16
SLOTS = 128 // HALO

MESH = pl.DeviceIdType.MESH
FLOAT = jnp.float32
HALF = jnp.bfloat16


def basis(total, modes):
    cells = np.arange(total, dtype=np.int64)
    order = np.arange(modes, dtype=np.int64)
    half = modes // 2
    wave = np.where(order < half, order, order - half + 1)
    phase = (cells[:, None] * wave[None, :] % total).astype(np.float64) * (2.0 * math.pi / total)
    return np.where(order[None, :] < half, np.cos(phase), np.sin(phase))


def halves(table):
    high = table.astype(ml_dtypes.bfloat16)
    low = (table - high.astype(np.float64)).astype(ml_dtypes.bfloat16)
    return high, low


def lon_table(total, count):
    chips, own = count // 2, KX // count
    table = basis(total, KX).T.reshape(chips, 2, own, chips, total // chips).transpose(3, 1, 0, 2, 4)
    return np.stack(halves(table.reshape(count, KX // 2, total // chips)), axis=1)


def lat_table(total, count, scale):
    table = (scale * basis(total, KY)).reshape(total, count, KY // count).transpose(1, 0, 2)
    return np.stack(halves(table), axis=1)


def split(x):
    high = x.astype(HALF)
    return high, (x - high.astype(FLOAT)).astype(HALF)


def turn(x, shift, axis):
    shift %= x.shape[axis]
    return x if shift == 0 else pltpu.roll(x, shift, axis)


def kernel(
    lon_count, lat_count,
    state_hbm, depth_hbm, source_hbm, gauge_lat_hbm, gauge_lon_hbm, misfit_hbm, lon_hbm, lat_hbm,
    fields, modes,
    source, gauge_lat, gauge_lon, misfit,
    ext, ext_depth, coef, gauges, pack_w, pack_e, got_e, got_w, lon_tab, lat_tab,
    shared, part, pieces, gathered,
    halo_send, halo_recv, in_sem, sh_send, sh_recv, rs_send, rs_recv, ga_send, ga_recv,
):
    rows, cols = depth_hbm.shape
    high, wide = rows + 2 * HALO, 2 * cols
    own = modes.shape[1]
    lon = lax.axis_index("lon")
    lat = lax.axis_index("lat")
    chips = lon_count // 2
    chip, core = lon // 2, lax.rem(lon, 2)
    partner = lon + 1 - 2 * core
    beside = lon - 1 + 2 * core
    has_beside = jnp.logical_and(beside >= 0, beside < lon_count)
    has_e, has_w = lon < lon_count - 1, lon > 0
    has_n, has_s = lat < lat_count - 1, lat > 0

    state = ext.at[:, :, 0:rows, 0:cols]
    depth = ext_depth.at[0:rows, 0:cols]
    pairs = [
        (state_hbm, state), (depth_hbm, depth), (source_hbm, source), (gauge_lat_hbm, gauge_lat),
        (gauge_lon_hbm, gauge_lon), (misfit_hbm, misfit), (lon_hbm.at[lon], lon_tab), (lat_hbm.at[lat], lat_tab),
    ]
    loads = [pltpu.make_async_copy(a, b, in_sem.at[i]) for i, (a, b) in enumerate(pairs)]
    for copy in loads:
        copy.start()

    corners = [
        (jnp.logical_and(has_e, has_n), 1, 1),
        (jnp.logical_and(has_e, has_s), 1, -1),
        (jnp.logical_and(has_w, has_n), -1, 1),
        (jnp.logical_and(has_w, has_s), -1, -1),
    ]
    barrier = pltpu.get_barrier_semaphore()
    pl.semaphore_signal(barrier, 1, device_id=(partner, lat), device_id_type=MESH)

    @pl.when(has_beside)
    def _():
        pl.semaphore_signal(barrier, 1, device_id=(beside, lat), device_id_type=MESH)

    for d in range(1, chips):
        target = 2 * lax.rem(chip + d, chips) + core
        pl.semaphore_signal(barrier, 1, device_id=(target, lat), device_id_type=MESH)
    for d in range(1, lat_count):
        pl.semaphore_signal(barrier, 1, device_id=(lon, lax.rem(lat + d, lat_count)), device_id_type=MESH)
    for there, dx, dy in corners:
        @pl.when(there)
        def _():
            pl.semaphore_signal(barrier, 1, device_id=(lon + dx, lat + dy), device_id_type=MESH)

    for copy in loads[2:6]:
        copy.wait()
    row = lax.broadcasted_iota(jnp.int32, (high, wide), 0)
    col = lax.broadcasted_iota(jnp.int32, (high, wide), 1)
    row = lat * rows + jnp.where(row < rows + HALO, row, row - high)
    real = jnp.logical_or(col < cols + HALO, col >= wide - HALO)
    col = lon * cols + jnp.where(col < cols + HALO, col, col - wide)
    inside = (row >= 0) & (row < lat_count * rows) & (col >= 0) & (col < lon_count * cols) & real
    coef[0] = jnp.where(inside, 0.25, 0.0).astype(FLOAT)
    for a in range(ADJ):
        hit = (row == gauge_lat[a]) & (col == gauge_lon[a]) & real
        gauges[a] = jnp.where(hit, 1.0, 0.0).astype(FLOAT)
    line = lax.broadcasted_iota(jnp.int32, (rows, cols), 0)
    place = lax.broadcasted_iota(jnp.int32, (rows, cols), 1)
    mask = jnp.zeros((rows, cols), FLOAT)
    side = rows // source.shape[0]
    for i in range(source.shape[0]):
        for j in range(source.shape[1]):
            tile = (line >= i * side) & (line < (i + 1) * side) & (place >= j * side) & (place < (j + 1) * side)
            mask = jnp.where(tile, source[i, j].astype(FLOAT), mask)

    for copy in loads[:2]:
        copy.wait()

    diagonal = sum(there.astype(jnp.int32) for there, _, _ in corners)
    pl.semaphore_wait(barrier, chips + lat_count - 1 + has_beside.astype(jnp.int32) + diagonal)

    low = slice(0, HALO)
    top = slice(rows - HALO, rows)
    north = slice(rows, rows + HALO)
    south = slice(rows + HALO, high)
    every = slice(0, rows)
    plan = [
        (has_e, has_w, pack_e, got_w.at[every], 1, 0),
        (has_w, has_e, pack_w, got_e.at[every], -1, 0),
        (has_n, has_s, ext.at[:, :, top, 0:cols], ext.at[:, :, south, 0:cols], 0, 1),
        (has_s, has_n, ext.at[:, :, low, 0:cols], ext.at[:, :, north, 0:cols], 0, -1),
        (has_n, has_s, ext_depth.at[top, 0:cols], ext_depth.at[south, 0:cols], 0, 1),
        (has_s, has_n, ext_depth.at[low, 0:cols], ext_depth.at[north, 0:cols], 0, -1),
        (corners[0][0], corners[3][0], pack_e.at[top], got_w.at[south], 1, 1),
        (corners[1][0], corners[2][0], pack_e.at[low], got_w.at[north], 1, -1),
        (corners[2][0], corners[1][0], pack_w.at[top], got_e.at[south], -1, 1),
        (corners[3][0], corners[0][0], pack_w.at[low], got_e.at[north], -1, -1),
    ]

    def halo_copy(index):
        _, _, source_ref, target, dx, dy = plan[index]
        return pltpu.make_async_remote_copy(
            src_ref=source_ref, dst_ref=target,
            send_sem=halo_send.at[index], recv_sem=halo_recv.at[index],
            device_id=(lon + dx, lat + dy), device_id_type=MESH,
        )

    def halo_start(indices):
        for index in indices:
            @pl.when(plan[index][0])
            def _():
                halo_copy(index).start()

    halo_start((2, 3, 4, 5))

    lane = lax.broadcasted_iota(jnp.int32, (rows, 128), 1)
    arrays = [ext[f, a, 0:rows, 0:cols] for f in range(3) for a in range(ADJ)] + [ext_depth[0:rows, 0:cols]]
    for tile in range(2):
        west = jnp.zeros((rows, 128), FLOAT)
        east = west
        for slot in range(SLOTS):
            index = tile * SLOTS + slot
            if index < len(arrays):
                at = slot * HALO
                here = jnp.logical_and(lane >= at, lane < at + HALO)
                west = jnp.where(here, turn(arrays[index], at, 1), west)
                east = jnp.where(here, turn(arrays[index], at + HALO - cols, 1), east)
        pack_w[:, tile * 128:(tile + 1) * 128] = west
        pack_e[:, tile * 128:(tile + 1) * 128] = east

    halo_start((6, 7, 8, 9, 0, 1))
    for _, gets, _, target, _, _ in plan:
        @pl.when(jnp.logical_not(gets))
        def _():
            target[...] = jnp.zeros(target.shape, FLOAT)

    for index, (_, gets, _, _, _, _) in enumerate(plan):
        @pl.when(gets)
        def _():
            halo_copy(index).wait_recv()

    for index in (2, 3):
        @pl.when(plan[index][0])
        def _():
            halo_copy(index).wait_send()

    lane = lax.broadcasted_iota(jnp.int32, (high, 128), 1)

    def unpacked(index):
        tile, at = index // SLOTS, index % SLOTS * HALO
        span = slice(tile * 128, (tile + 1) * 128)
        right = turn(got_e[:, span], -at, 1)
        left = turn(got_w[:, span], -at - HALO, 1)
        return jnp.where(lane < HALO, right, jnp.where(lane >= 128 - HALO, left, 0.0))

    ext_depth[:, cols:wide] = unpacked(3 * ADJ)
    quarter = 0.25 * ext_depth[...]
    coef[1] = turn(quarter, -1, 1)
    coef[2] = turn(quarter, -1, 0)

    def sh_copy(p):
        return pltpu.make_async_remote_copy(
            src_ref=shared.at[p, core], dst_ref=shared.at[p, core],
            send_sem=sh_send.at[p], recv_sem=sh_recv.at[p],
            device_id=(partner, lat), device_id_type=MESH,
        )

    def sh_arrival(p):
        return pltpu.make_async_remote_copy(
            src_ref=shared.at[p, 1 - core], dst_ref=shared.at[p, 1 - core],
            send_sem=sh_send.at[p], recv_sem=sh_recv.at[p],
            device_id=(partner, lat), device_id_type=MESH,
        )

    def rs_copy(p, d):
        target = lax.rem(chip + d, chips)
        return pltpu.make_async_remote_copy(
            src_ref=part.at[p, pl.ds(pl.multiple_of(target * own, own), own)],
            dst_ref=pieces.at[p, d - 1],
            send_sem=rs_send.at[p, d - 1], recv_sem=rs_recv.at[p, d - 1],
            device_id=(2 * target + core, lat), device_id_type=MESH,
        )

    def ga_copy(p, d):
        return pltpu.make_async_remote_copy(
            src_ref=gathered.at[p, lat], dst_ref=gathered.at[p, lat],
            send_sem=ga_send.at[p, d - 1], recv_sem=ga_recv.at[p, d - 1],
            device_id=(lon, lax.rem(lat + d, lat_count)), device_id_type=MESH,
        )

    def ga_arrival(p, d):
        origin = lax.rem(lat + lat_count - d, lat_count)
        return pltpu.make_async_remote_copy(
            src_ref=gathered.at[p, origin], dst_ref=gathered.at[p, origin],
            send_sem=ga_send.at[p, d - 1], recv_sem=ga_recv.at[p, d - 1],
            device_id=(lon, origin), device_id_type=MESH,
        )

    def prepare(p):
        for a in (2 * p, 2 * p + 1):
            ext[0, a, :, cols:wide] = unpacked(a)
            ext[1, a, :, cols:wide] = unpacked(ADJ + a)
            ext[2, a, :, cols:wide] = unpacked(2 * ADJ + a)
            ext[1, a] = turn(ext[1, a], -1, 1)
            ext[2, a] = turn(ext[2, a], -1, 0)

    def advance(p, first, last):
        def step(t, carry):
            for a in (2 * p, 2 * p + 1):
                east, north_ = ext[1, a], ext[2, a]
                change = (east - turn(east, 2, 1)) + (north_ - turn(north_, 2, 0))
                height = ext[0, a] + coef[0] * change + gauges[a] * misfit[a, t]
                ext[0, a] = height
                ext[1, a] = east + coef[1] * (turn(height, -2, 1) - height)
                ext[2, a] = north_ + coef[2] * (turn(height, -2, 0) - height)
            return carry

        lax.fori_loop(first, last, step, 0)

    def share(p):
        masked = [ext[0, a, 0:rows, 0:cols] * mask for a in (2 * p, 2 * p + 1)]
        shared[p, core] = jnp.concatenate(masked, axis=0)
        sh_copy(p).start()

    def finish(p):
        for a in (2 * p, 2 * p + 1):
            fields[0, a] = ext[0, a, 0:rows, 0:cols]
            fields[1, a] = turn(ext[1, a], 1, 1)[0:rows, 0:cols]
            fields[2, a] = turn(ext[2, a], 1, 0)[0:rows, 0:cols]

    def project(p):
        sh_arrival(p).wait_recv()
        high_m, low_m = split(jnp.concatenate([shared[p, 0], shared[p, 1]], axis=1))
        dims = (((1,), (1,)), ((), ()))
        part[p] = (
            lax.dot_general(lon_tab[0], high_m, dims, preferred_element_type=FLOAT)
            + lax.dot_general(lon_tab[0], low_m, dims, preferred_element_type=FLOAT)
            + lax.dot_general(lon_tab[1], high_m, dims, preferred_element_type=FLOAT)
        )
        for d in range(1, chips):
            rs_copy(p, d).start()

    prepare(0)
    advance(0, 0, STEPS)
    share(0)
    for copy in loads[6:]:
        copy.wait()
    prepare(1)
    advance(1, 0, STEPS // 2)
    project(0)
    advance(1, STEPS // 2, STEPS)
    share(1)
    finish(0)
    finish(1)
    project(1)

    for p in range(PAIRS):
        total = part[p, pl.ds(pl.multiple_of(chip * own, own), own)]
        for d in range(1, chips):
            rs_copy(p, d).wait_recv()
            total = total + pieces[p, d - 1]
        gathered[p, lat] = total
        for d in range(1, lat_count):
            ga_copy(p, d).start()

    blocks = [slice(z * rows, (z + 1) * rows) for z in range(lat_count) for _ in range(2)]
    by_high = jnp.concatenate([lat_tab[0, block] for block in blocks], axis=0)
    by_low = jnp.concatenate([lat_tab[1, block] for block in blocks], axis=0)
    first = lax.broadcasted_iota(jnp.int32, (own, 2 * rows), 1) < rows
    for p in range(PAIRS):
        for d in range(1, lat_count):
            ga_arrival(p, d).wait_recv()
        sums = [gathered[p, z] for z in range(lat_count)]
        high_g, low_g = split(
            jnp.concatenate(
                [
                    jnp.concatenate([jnp.where(first, x, 0.0) for x in sums], axis=1),
                    jnp.concatenate([jnp.where(first, 0.0, x) for x in sums], axis=1),
                ],
                axis=0,
            )
        )
        result = (
            jnp.dot(high_g, by_high, preferred_element_type=FLOAT)
            + jnp.dot(low_g, by_high, preferred_element_type=FLOAT)
            + jnp.dot(high_g, by_low, preferred_element_type=FLOAT)
        )
        for member in range(2):
            modes[2 * p + member] = result[member * own:(member + 1) * own]

    for index in (0, 1, 4, 5, 6, 7, 8, 9):
        @pl.when(plan[index][0])
        def _():
            halo_copy(index).wait_send()
    for p in range(PAIRS):
        sh_copy(p).wait_send()
        for d in range(1, chips):
            rs_copy(p, d).wait_send()
        for d in range(1, lat_count):
            ga_copy(p, d).wait_send()


def on_device(lon_count, lat_count, tables, state, depth, source_mask, gauge_lat, gauge_lon, misfit):
    rows, cols = depth.shape
    own_x, own_y = KX // lon_count, KY // lat_count
    high, wide = rows + 2 * HALO, 2 * cols
    vmem = pl.BlockSpec(memory_space=pltpu.VMEM)
    hbm = pl.BlockSpec(memory_space=pltpu.HBM)
    dma = pltpu.SemaphoreType.DMA
    return pl.pallas_call(
        functools.partial(kernel, lon_count, lat_count),
        out_shape=(
            jax.ShapeDtypeStruct((3, ADJ, rows, cols), FLOAT),
            jax.ShapeDtypeStruct((ADJ, own_x, own_y), FLOAT),
        ),
        in_specs=[hbm] * 8,
        out_specs=(vmem, vmem),
        scratch_shapes=[
            pltpu.SMEM(source_mask.shape, jnp.int32),
            pltpu.SMEM((ADJ,), jnp.int32),
            pltpu.SMEM((ADJ,), jnp.int32),
            pltpu.SMEM((ADJ, STEPS), FLOAT),
            pltpu.VMEM((3, ADJ, high, wide), FLOAT),
            pltpu.VMEM((high, wide), FLOAT),
            pltpu.VMEM((3, high, wide), FLOAT),
            pltpu.VMEM((ADJ, high, wide), FLOAT),
            pltpu.VMEM((rows, 256), FLOAT),
            pltpu.VMEM((rows, 256), FLOAT),
            pltpu.VMEM((high, 256), FLOAT),
            pltpu.VMEM((high, 256), FLOAT),
            pltpu.VMEM((2, KX // 2, 2 * cols), HALF),
            pltpu.VMEM((2, lat_count * rows, own_y), HALF),
            pltpu.VMEM((PAIRS, 2, 2 * rows, cols), FLOAT),
            pltpu.VMEM((PAIRS, KX // 2, 2 * rows), FLOAT),
            pltpu.VMEM((PAIRS, lon_count // 2 - 1, own_x, 2 * rows), FLOAT),
            pltpu.VMEM((PAIRS, lat_count, own_x, 2 * rows), FLOAT),
            dma((10,)),
            dma((10,)),
            dma((8,)),
            dma((PAIRS,)),
            dma((PAIRS,)),
            dma((PAIRS, lon_count // 2 - 1)),
            dma((PAIRS, lon_count // 2 - 1)),
            dma((PAIRS, lat_count - 1)),
            dma((PAIRS, lat_count - 1)),
        ],
        compiler_params=pltpu.CompilerParams(
            collective_id=0, has_side_effects=True, vmem_limit_bytes=32 * 1024 * 1024
        ),
    )(*[pltpu.with_memory_space_constraint(x, pltpu.HBM) for x in (state, depth, source_mask, gauge_lat, gauge_lon, misfit.T, *tables)])


def solution(mesh):
    lon_count, lat_count = mesh.shape["lon"], mesh.shape["lat"]
    placed = (P(None, None, "lat", "lon"), P("lat", "lon"), P("lat", "lon"), P(), P(), P())

    def whole(state, depth, source_mask, gauge_lat, gauge_lon, misfit):
        total_rows, total_cols = depth.shape
        scale = 2.0 / math.sqrt(total_rows * total_cols)
        tables = (lon_table(total_cols, lon_count), lat_table(total_rows, lat_count, scale))

        def local(*args):
            constants = tuple(jnp.asarray(table) for table in tables)
            return on_device(lon_count, lat_count, constants, *args)

        return jax.shard_map(
            local,
            mesh=mesh,
            in_specs=placed,
            out_specs=(P(None, None, "lat", "lon"), P(None, "lon", "lat")),
            check_vma=False,
        )(state, depth, source_mask, gauge_lat, gauge_lon, misfit)

    return whole
```

```python
import functools
import math

import jax
import jax.numpy as jnp
import ml_dtypes
import numpy as np
from jax import lax
from jax.experimental import pallas as pl
from jax.experimental.pallas import tpu as pltpu
from jax.sharding import PartitionSpec as P

STEPS = 6
KX = 512
KY = 512
ADJ = 4
PAIRS = ADJ // 2
SPLIT = 2
HALO = 16
REACH = 2 * STEPS
SLOTS = 128 // HALO

MESH = pl.DeviceIdType.MESH
FLOAT = jnp.float32
HALF = jnp.bfloat16


def basis(total, modes):
    cells = np.arange(total, dtype=np.int64)
    order = np.arange(modes, dtype=np.int64)
    half = modes // 2
    wave = np.where(order < half, order, order - half + 1)
    phase = (cells[:, None] * wave[None, :] % total).astype(np.float64) * (2.0 * math.pi / total)
    return np.where(order[None, :] < half, np.cos(phase), np.sin(phase))


def halves(table):
    high = table.astype(ml_dtypes.bfloat16)
    low = (table - high.astype(np.float64)).astype(ml_dtypes.bfloat16)
    return high, low


def lon_table(total, count):
    chips, own = count // 2, KX // count
    table = basis(total, KX).T.reshape(chips, 2, own, chips, total // chips).transpose(3, 1, 0, 2, 4)
    return np.stack(halves(table.reshape(count, KX // 2, total // chips)), axis=1)


def lat_table(total, count, scale):
    table = (scale * basis(total, KY)).reshape(total, count, KY // count).transpose(1, 0, 2)
    return np.stack(halves(table), axis=1)


def split(x):
    high = x.astype(HALF)
    return high, (x - high.astype(FLOAT)).astype(HALF)


def turn(x, shift, axis):
    shift %= x.shape[axis]
    return x if shift == 0 else pltpu.roll(x, shift, axis)


def kernel(
    lon_count, lat_count,
    state_hbm, depth_hbm, source_hbm, gauge_lat_hbm, gauge_lon_hbm, misfit_hbm, lon_hbm, lat_hbm,
    fields, modes,
    source, gauge_lat, gauge_lon, misfit,
    ext, ext_depth, coef, gauges, pack_w, pack_e, pack_n, pack_s, got_e, got_w, got_n, got_s, lon_tab, lat_tab,
    shared, part, pieces, gathered,
    halo_send, halo_recv, in_sem, sh_send, sh_recv, rs_send, rs_recv, ga_send, ga_recv,
):
    rows, cols = depth_hbm.shape
    high, wide = rows + 2 * HALO, 2 * cols
    own = modes.shape[1]
    lon = lax.axis_index("lon")
    lat = lax.axis_index("lat")
    chips = lon_count // 2
    chip, core = lon // 2, lax.rem(lon, 2)
    partner = lon + 1 - 2 * core
    beside = lon - 1 + 2 * core
    has_beside = jnp.logical_and(beside >= 0, beside < lon_count)
    has_e, has_w = lon < lon_count - 1, lon > 0
    has_n, has_s = lat < lat_count - 1, lat > 0

    state = ext.at[:, :, 0:rows, 0:cols]
    depth = ext_depth.at[0:rows, 0:cols]
    pairs = [
        (state_hbm, state), (depth_hbm, depth), (source_hbm, source), (gauge_lat_hbm, gauge_lat),
        (gauge_lon_hbm, gauge_lon), (misfit_hbm, misfit), (lon_hbm.at[lon], lon_tab), (lat_hbm.at[lat], lat_tab),
    ]
    loads = [pltpu.make_async_copy(a, b, in_sem.at[i]) for i, (a, b) in enumerate(pairs)]
    for copy in loads:
        copy.start()

    corners = [
        (jnp.logical_and(has_e, has_n), 1, 1),
        (jnp.logical_and(has_e, has_s), 1, -1),
        (jnp.logical_and(has_w, has_n), -1, 1),
        (jnp.logical_and(has_w, has_s), -1, -1),
    ]
    barrier = pltpu.get_barrier_semaphore()
    pl.semaphore_signal(barrier, 1, device_id=(partner, lat), device_id_type=MESH)

    @pl.when(has_beside)
    def _():
        pl.semaphore_signal(barrier, 1, device_id=(beside, lat), device_id_type=MESH)

    for d in range(1, chips):
        target = 2 * lax.rem(chip + d, chips) + core
        pl.semaphore_signal(barrier, 1, device_id=(target, lat), device_id_type=MESH)
    for d in range(1, lat_count):
        pl.semaphore_signal(barrier, 1, device_id=(lon, lax.rem(lat + d, lat_count)), device_id_type=MESH)
    for there, dx, dy in corners:
        @pl.when(there)
        def _():
            pl.semaphore_signal(barrier, 1, device_id=(lon + dx, lat + dy), device_id_type=MESH)

    for copy in loads[2:6]:
        copy.wait()
    row = lax.broadcasted_iota(jnp.int32, (high, wide), 0)
    col = lax.broadcasted_iota(jnp.int32, (high, wide), 1)
    row = lat * rows + jnp.where(row < rows + HALO, row, row - high)
    real = jnp.logical_or(col < cols + HALO, col >= wide - HALO)
    col = lon * cols + jnp.where(col < cols + HALO, col, col - wide)
    inside = (row >= 0) & (row < lat_count * rows) & (col >= 0) & (col < lon_count * cols) & real
    coef[0] = jnp.where(inside, 0.25, 0.0).astype(FLOAT)
    for a in range(ADJ):
        hit = (row == gauge_lat[a]) & (col == gauge_lon[a]) & real
        gauges[a] = jnp.where(hit, 1.0, 0.0).astype(FLOAT)
    line = lax.broadcasted_iota(jnp.int32, (rows, cols), 0)
    place = lax.broadcasted_iota(jnp.int32, (rows, cols), 1)
    mask = jnp.zeros((rows, cols), FLOAT)
    side = rows // source.shape[0]
    for i in range(source.shape[0]):
        for j in range(source.shape[1]):
            tile = (line >= i * side) & (line < (i + 1) * side) & (place >= j * side) & (place < (j + 1) * side)
            mask = jnp.where(tile, source[i, j].astype(FLOAT), mask)

    for copy in loads[:2]:
        copy.wait()

    diagonal = sum(there.astype(jnp.int32) for there, _, _ in corners)
    pl.semaphore_wait(barrier, chips + lat_count - 1 + has_beside.astype(jnp.int32) + diagonal)

    low = slice(0, HALO)
    top = slice(rows - HALO, rows)
    north = slice(rows, rows + HALO)
    south = slice(rows + HALO, high)
    every = slice(0, rows)
    plan = [
        (has_e, has_w, pack_e, got_w.at[every], 1, 0),
        (has_w, has_e, pack_w, got_e.at[every], -1, 0),
        (has_n, has_s, pack_n, got_s, 0, 1),
        (has_s, has_n, pack_s, got_n, 0, -1),
        (corners[0][0], corners[3][0], pack_e.at[top], got_w.at[south], 1, 1),
        (corners[1][0], corners[2][0], pack_e.at[low], got_w.at[north], 1, -1),
        (corners[2][0], corners[1][0], pack_w.at[top], got_e.at[south], -1, 1),
        (corners[3][0], corners[0][0], pack_w.at[low], got_e.at[north], -1, -1),
    ]

    def halo_copy(index):
        _, _, source_ref, target, dx, dy = plan[index]
        return pltpu.make_async_remote_copy(
            src_ref=source_ref, dst_ref=target,
            send_sem=halo_send.at[index], recv_sem=halo_recv.at[index],
            device_id=(lon + dx, lat + dy), device_id_type=MESH,
        )

    def halo_start(indices):
        for index in indices:
            @pl.when(plan[index][0])
            def _():
                halo_copy(index).start()

    arrays = [ext.at[f, a] for f in range(3) for a in range(ADJ)] + [ext_depth]
    for index, array in enumerate(arrays):
        span = slice(index * REACH, (index + 1) * REACH)
        pack_n[span] = array[rows - REACH:rows, 0:cols]
        pack_s[span] = array[0:REACH, 0:cols]
    for pack in (pack_n, pack_s):
        pack[len(arrays) * REACH:] = jnp.zeros((pack.shape[0] - len(arrays) * REACH, cols), FLOAT)
    halo_start((2, 3))

    lane = lax.broadcasted_iota(jnp.int32, (rows, 128), 1)
    for tile in range(2):
        west = jnp.zeros((rows, 128), FLOAT)
        east = west
        for slot in range(SLOTS):
            index = tile * SLOTS + slot
            if index < len(arrays):
                at = slot * HALO
                here = jnp.logical_and(lane >= at, lane < at + HALO)
                west = jnp.where(here, turn(arrays[index][0:rows, 0:cols], at, 1), west)
                east = jnp.where(here, turn(arrays[index][0:rows, 0:cols], at + HALO - cols, 1), east)
        pack_w[:, tile * 128:(tile + 1) * 128] = west
        pack_e[:, tile * 128:(tile + 1) * 128] = east

    halo_start((4, 5, 6, 7, 0, 1))
    for _, gets, _, target, _, _ in plan:
        @pl.when(jnp.logical_not(gets))
        def _():
            target[...] = jnp.zeros(target.shape, FLOAT)

    for index, (_, gets, _, _, _, _) in enumerate(plan):
        @pl.when(gets)
        def _():
            halo_copy(index).wait_recv()

    for index, array in enumerate(arrays):
        span = slice(index * REACH, (index + 1) * REACH)
        array[rows:rows + REACH, 0:cols] = got_n[span]
        array[rows + REACH:high - REACH, 0:cols] = jnp.zeros((high - rows - 2 * REACH, cols), FLOAT)
        array[high - REACH:high, 0:cols] = got_s[span]

    lane = lax.broadcasted_iota(jnp.int32, (high, 128), 1)

    def unpacked(index):
        tile, at = index // SLOTS, index % SLOTS * HALO
        span = slice(tile * 128, (tile + 1) * 128)
        right = turn(got_e[:, span], -at, 1)
        left = turn(got_w[:, span], -at - HALO, 1)
        return jnp.where(lane < HALO, right, jnp.where(lane >= 128 - HALO, left, 0.0))

    ext_depth[:, cols:wide] = unpacked(3 * ADJ)
    quarter = 0.25 * ext_depth[...]
    coef[1] = turn(quarter, -1, 1)
    coef[2] = turn(quarter, -1, 0)

    def sh_copy(p):
        return pltpu.make_async_remote_copy(
            src_ref=shared.at[p, core], dst_ref=shared.at[p, core],
            send_sem=sh_send.at[p], recv_sem=sh_recv.at[p],
            device_id=(partner, lat), device_id_type=MESH,
        )

    def sh_arrival(p):
        return pltpu.make_async_remote_copy(
            src_ref=shared.at[p, 1 - core], dst_ref=shared.at[p, 1 - core],
            send_sem=sh_send.at[p], recv_sem=sh_recv.at[p],
            device_id=(partner, lat), device_id_type=MESH,
        )

    def rs_copy(p, d):
        target = lax.rem(chip + d, chips)
        return pltpu.make_async_remote_copy(
            src_ref=part.at[p, pl.ds(pl.multiple_of(target * own, own), own)],
            dst_ref=pieces.at[p, d - 1],
            send_sem=rs_send.at[p, d - 1], recv_sem=rs_recv.at[p, d - 1],
            device_id=(2 * target + core, lat), device_id_type=MESH,
        )

    def ga_copy(p, d):
        return pltpu.make_async_remote_copy(
            src_ref=gathered.at[p, lat], dst_ref=gathered.at[p, lat],
            send_sem=ga_send.at[p, d - 1], recv_sem=ga_recv.at[p, d - 1],
            device_id=(lon, lax.rem(lat + d, lat_count)), device_id_type=MESH,
        )

    def ga_arrival(p, d):
        origin = lax.rem(lat + lat_count - d, lat_count)
        return pltpu.make_async_remote_copy(
            src_ref=gathered.at[p, origin], dst_ref=gathered.at[p, origin],
            send_sem=ga_send.at[p, d - 1], recv_sem=ga_recv.at[p, d - 1],
            device_id=(lon, origin), device_id_type=MESH,
        )

    def prepare(p):
        for a in (2 * p, 2 * p + 1):
            ext[0, a, :, cols:wide] = unpacked(a)
            ext[1, a, :, cols:wide] = unpacked(ADJ + a)
            ext[2, a, :, cols:wide] = unpacked(2 * ADJ + a)
            ext[1, a] = turn(ext[1, a], -1, 1)
            ext[2, a] = turn(ext[2, a], -1, 0)

    def advance(p, first, last):
        def step(t, carry):
            for a in (2 * p, 2 * p + 1):
                east, north_ = ext[1, a], ext[2, a]
                change = (east - turn(east, 2, 1)) + (north_ - turn(north_, 2, 0))
                height = ext[0, a] + coef[0] * change + gauges[a] * misfit[a, t]
                ext[0, a] = height
                ext[1, a] = east + coef[1] * (turn(height, -2, 1) - height)
                ext[2, a] = north_ + coef[2] * (turn(height, -2, 0) - height)
            return carry

        lax.fori_loop(first, last, step, 0)

    def share(p):
        masked = [ext[0, a, 0:rows, 0:cols] * mask for a in (2 * p, 2 * p + 1)]
        shared[p, core] = jnp.concatenate(masked, axis=0)
        sh_copy(p).start()

    def finish(p):
        for a in (2 * p, 2 * p + 1):
            fields[0, a] = ext[0, a, 0:rows, 0:cols]
            fields[1, a] = turn(ext[1, a], 1, 1)[0:rows, 0:cols]
            fields[2, a] = turn(ext[2, a], 1, 0)[0:rows, 0:cols]

    def project(p):
        sh_arrival(p).wait_recv()
        high_m, low_m = split(jnp.concatenate([shared[p, 0], shared[p, 1]], axis=1))
        dims = (((1,), (1,)), ((), ()))
        part[p] = (
            lax.dot_general(lon_tab[0], high_m, dims, preferred_element_type=FLOAT)
            + lax.dot_general(lon_tab[0], low_m, dims, preferred_element_type=FLOAT)
            + lax.dot_general(lon_tab[1], high_m, dims, preferred_element_type=FLOAT)
        )
        for d in range(1, chips):
            rs_copy(p, d).start()

    def collect(p):
        total = part[p, pl.ds(pl.multiple_of(chip * own, own), own)]
        for d in range(1, chips):
            rs_copy(p, d).wait_recv()
            total = total + pieces[p, d - 1]
        gathered[p, lat] = total
        for d in range(1, lat_count):
            ga_copy(p, d).start()

    blocks = [slice(z * rows, (z + 1) * rows) for z in range(lat_count) for _ in range(2)]
    first = lax.broadcasted_iota(jnp.int32, (own, 2 * rows), 1) < rows

    def conclude(p):
        by_high = jnp.concatenate([lat_tab[0, block] for block in blocks], axis=0)
        by_low = jnp.concatenate([lat_tab[1, block] for block in blocks], axis=0)
        for d in range(1, lat_count):
            ga_arrival(p, d).wait_recv()
        sums = [gathered[p, z] for z in range(lat_count)]
        high_g, low_g = split(
            jnp.concatenate(
                [
                    jnp.concatenate([jnp.where(first, x, 0.0) for x in sums], axis=1),
                    jnp.concatenate([jnp.where(first, 0.0, x) for x in sums], axis=1),
                ],
                axis=0,
            )
        )
        result = (
            jnp.dot(high_g, by_high, preferred_element_type=FLOAT)
            + jnp.dot(low_g, by_high, preferred_element_type=FLOAT)
            + jnp.dot(high_g, by_low, preferred_element_type=FLOAT)
        )
        for member in range(2):
            modes[2 * p + member] = result[member * own:(member + 1) * own]

    prepare(0)
    advance(0, 0, STEPS)
    share(0)
    for copy in loads[6:]:
        copy.wait()
    prepare(1)
    advance(1, 0, SPLIT)
    project(0)
    advance(1, SPLIT, STEPS)
    share(1)
    finish(0)
    project(1)
    collect(0)
    finish(1)
    collect(1)
    conclude(0)
    conclude(1)

    for index in range(len(plan)):
        @pl.when(plan[index][0])
        def _():
            halo_copy(index).wait_send()
    for p in range(PAIRS):
        sh_copy(p).wait_send()
        for d in range(1, chips):
            rs_copy(p, d).wait_send()
        for d in range(1, lat_count):
            ga_copy(p, d).wait_send()


def on_device(lon_count, lat_count, tables, state, depth, source_mask, gauge_lat, gauge_lon, misfit):
    rows, cols = depth.shape
    own_x, own_y = KX // lon_count, KY // lat_count
    high, wide = rows + 2 * HALO, 2 * cols
    vmem = pl.BlockSpec(memory_space=pltpu.VMEM)
    hbm = pl.BlockSpec(memory_space=pltpu.HBM)
    dma = pltpu.SemaphoreType.DMA
    strip = ((3 * ADJ + 1) * REACH + 4, cols)
    return pl.pallas_call(
        functools.partial(kernel, lon_count, lat_count),
        out_shape=(
            jax.ShapeDtypeStruct((3, ADJ, rows, cols), FLOAT),
            jax.ShapeDtypeStruct((ADJ, own_x, own_y), FLOAT),
        ),
        in_specs=[hbm] * 8,
        out_specs=(vmem, vmem),
        scratch_shapes=[
            pltpu.SMEM(source_mask.shape, jnp.int32),
            pltpu.SMEM((ADJ,), jnp.int32),
            pltpu.SMEM((ADJ,), jnp.int32),
            pltpu.SMEM((ADJ, STEPS), FLOAT),
            pltpu.VMEM((3, ADJ, high, wide), FLOAT),
            pltpu.VMEM((high, wide), FLOAT),
            pltpu.VMEM((3, high, wide), FLOAT),
            pltpu.VMEM((ADJ, high, wide), FLOAT),
            pltpu.VMEM((rows, 256), FLOAT),
            pltpu.VMEM((rows, 256), FLOAT),
            pltpu.VMEM(strip, FLOAT),
            pltpu.VMEM(strip, FLOAT),
            pltpu.VMEM((high, 256), FLOAT),
            pltpu.VMEM((high, 256), FLOAT),
            pltpu.VMEM(strip, FLOAT),
            pltpu.VMEM(strip, FLOAT),
            pltpu.VMEM((2, KX // 2, 2 * cols), HALF),
            pltpu.VMEM((2, lat_count * rows, own_y), HALF),
            pltpu.VMEM((PAIRS, 2, 2 * rows, cols), FLOAT),
            pltpu.VMEM((PAIRS, KX // 2, 2 * rows), FLOAT),
            pltpu.VMEM((PAIRS, lon_count // 2 - 1, own_x, 2 * rows), FLOAT),
            pltpu.VMEM((PAIRS, lat_count, own_x, 2 * rows), FLOAT),
            dma((8,)),
            dma((8,)),
            dma((8,)),
            dma((PAIRS,)),
            dma((PAIRS,)),
            dma((PAIRS, lon_count // 2 - 1)),
            dma((PAIRS, lon_count // 2 - 1)),
            dma((PAIRS, lat_count - 1)),
            dma((PAIRS, lat_count - 1)),
        ],
        compiler_params=pltpu.CompilerParams(
            collective_id=0, has_side_effects=True, vmem_limit_bytes=32 * 1024 * 1024
        ),
    )(*[pltpu.with_memory_space_constraint(x, pltpu.HBM) for x in (state, depth, source_mask, gauge_lat, gauge_lon, misfit.T, *tables)])


def solution(mesh):
    lon_count, lat_count = mesh.shape["lon"], mesh.shape["lat"]
    placed = (P(None, None, "lat", "lon"), P("lat", "lon"), P("lat", "lon"), P(), P(), P())

    def whole(state, depth, source_mask, gauge_lat, gauge_lon, misfit):
        total_rows, total_cols = depth.shape
        scale = 2.0 / math.sqrt(total_rows * total_cols)
        tables = (lon_table(total_cols, lon_count), lat_table(total_rows, lat_count, scale))

        def local(*args):
            constants = tuple(jnp.asarray(table) for table in tables)
            return on_device(lon_count, lat_count, constants, *args)

        return jax.shard_map(
            local,
            mesh=mesh,
            in_specs=placed,
            out_specs=(P(None, None, "lat", "lon"), P(None, "lon", "lat")),
            check_vma=False,
        )(state, depth, source_mask, gauge_lat, gauge_lon, misfit)

    return whole
```
